32 devices in a mesh: ctx: 8 (over z, core), exp: 4 (over y, x).
Axes of the slice: x: 2, y: 2, z: 4, core: 2. Of those that a mesh axis runs over, the one named last changes fastest.
Arguments:
- tokens: bfloat16 [16384, 1024], P(('ctx', 'exp')), may hold values from -30 to 30
- slot_keys: bfloat16 [1024, 512], replicated, may hold values from -64 to 64
- expert_in: bfloat16 [16, 1024, 2048], P('exp'), may hold values from -0.1875 to 0.1875
- expert_out: bfloat16 [16, 2048, 1024], P('exp'), may hold values from -0.25 to 0.25
- slot_counts: int32 [32, 16], P(('ctx', 'exp')), may hold values from 0 to 64, as said below
- slot_reach: int32 [32, 8], P(('ctx', 'exp')), may hold values from 0 to 7, as said below
Outputs:
- mixed: bfloat16 [16384, 1024], P(('ctx', 'exp'))
The draws below stay inside these ranges and needn't reach their ends.
Inputs may be any that keep to these rules, and one draw needn't show every extreme that they name: `slot_counts`: row k gives, in expert order, how many of the 512 slots of window k each expert takes; every row sums to 512; one expert, the same in every row, takes exactly 64 slots in every row. `slot_reach`: entry [k, j] is the last token block read by slots j * 64 to (j + 1) * 64 - 1 of window k; every row holds a 0 and a 7.
All inputs are finite; a program needn't handle non-finite values.
Results may differ from the reference program's by a relative error of at most 0.012.
The reference program's roundings to bfloat16 on the way count: a program that leaves them out, or rounds other values in their place, can miss the bound.
Values may be sent and summed in bfloat16 or wider, within the bound.
A program may use at most 64 MiB of HBM per device.

```python
import math
import jax
import jax.numpy as jnp
from jax import lax

D = 1024
HID = 2048
E = 16
BLOCK = 64
SLOTS = 512
CAP = 64
TBLK = 8
WINDOWS = 32
TOKENS = 16384


def key_parts(key):
    key_base = jax.random.fold_in(key, 0)
    return key_base


def draw_slot_keys(key, part):
    key_base = key_parts(jax.random.fold_in(key, 3))
    spread = 2.0 / math.sqrt(D)
    base = spread * jnp.clip(jax.random.normal(key_base, (D, SLOTS), jnp.float32), -6.0, 6.0)
    return jnp.clip(base, -64.0, 64.0).astype(jnp.bfloat16)


def draw_tokens(key, part):
    key_main = jax.random.fold_in(jax.random.fold_in(key, 5), 0)
    values = jnp.clip(jax.random.normal(key_main, (TOKENS, D), jnp.float32), -6.0, 6.0)
    return jnp.clip(values, -30.0, 30.0).astype(jnp.bfloat16)


def permute_experts(subkey):
    return jax.random.permutation(subkey, E)


def permute_blocks(subkey):
    return jax.random.permutation(subkey, SLOTS // BLOCK)


def draw_slot_counts(key, part):
    key_hot, key_order, key_shift = jax.random.split(jax.random.fold_in(key, 7), 3)
    hottest = jax.random.randint(key_hot, (), 0, E)
    rank_table = jax.vmap(permute_experts)(jax.random.split(key_order, WINDOWS))
    rank_table = jnp.where(jnp.arange(E)[None, :] == hottest, -1, rank_table)
    expert_order = jnp.argsort(rank_table, axis=1, stable=True)
    half_count = (E - 2) // 2
    shifts = jax.random.randint(key_shift, (WINDOWS, half_count), -(CAP // 2 - 1), CAP // 2)
    values = jnp.concatenate([jnp.full((WINDOWS, 1), CAP, jnp.int32), jnp.zeros((WINDOWS, 1), jnp.int32), (CAP // 2 + shifts).astype(jnp.int32), (CAP // 2 - shifts).astype(jnp.int32)], axis=1)
    counts = jnp.zeros((WINDOWS, E), jnp.int32).at[jnp.arange(WINDOWS)[:, None], expert_order].set(values)
    return counts.astype(jnp.int32)


def draw_slot_reach(key, part):
    key_perm, key_level = jax.random.split(jax.random.fold_in(key, 9), 2)
    placement = jax.vmap(permute_blocks)(jax.random.split(key_perm, WINDOWS))
    levels = jax.random.randint(key_level, (WINDOWS, SLOTS // BLOCK), 0, TBLK)
    return jnp.where(placement == 0, 0, jnp.where(placement == 1, TBLK - 1, levels)).astype(jnp.int32)


def block_scale(rng, extent, pieces, least, high):
    level = 1.0
    for dim, blocks in pieces:
        heights = jax.random.uniform(jax.random.fold_in(jax.random.fold_in(rng, 6), dim), (blocks,), jnp.float32, least / len(pieces), high / len(pieces))
        level = level * jnp.repeat(jnp.exp(heights), extent[dim] // blocks).reshape((-1,) + (1,) * (len(extent) - 1 - dim))
    return level


def gaussian(stream_key, shape, scale, bound, shards=(), held_as=jnp.bfloat16):
    drawn = jax.random.normal(stream_key, shape, jnp.float32) * scale
    if len(shards) > 0:
        drawn = block_scale(stream_key, shape, shards, -0.22, 0.18) * drawn
    return jnp.clip(drawn, min=-bound, max=bound).astype(held_as)


def setup_inputs(seed: int = 0) -> dict:
    key_list = jax.random.split(jax.random.key(seed), 7)
    tokens = draw_tokens(jax.random.fold_in(key_list[6], 71), 0)
    slot_keys = draw_slot_keys(jax.random.fold_in(key_list[6], 71), 0)
    expert_in = gaussian(key_list[2], (E, D, HID), D ** -0.5, 0.1875, ((0, 4),))
    expert_out = gaussian(key_list[3], (E, HID, D), (HID // 4) ** -0.5, 0.25, ((0, 4),))
    slot_counts = draw_slot_counts(jax.random.fold_in(key_list[6], 71), 0)
    slot_reach = draw_slot_reach(jax.random.fold_in(key_list[6], 71), 0)
    return dict(tokens=tokens, slot_keys=slot_keys, expert_in=expert_in, expert_out=expert_out, slot_counts=slot_counts, slot_reach=slot_reach)


EPSILON = 1e-06

def normalize(values):
    floats = values.astype(jnp.float32)
    inverse_rms = lax.rsqrt(lax.optimization_barrier(jnp.mean(floats * floats, axis=-1, keepdims=True)) + EPSILON)
    return (floats * inverse_rms).astype(jnp.bfloat16)

def block_levels(reach_row, slot_count):
    block_count = reach_row.shape[0]
    block_width = slot_count // block_count
    return jnp.broadcast_to(reach_row[:, None], (block_count, block_width)).reshape(slot_count).astype(jnp.int32)

def token_levels(tok_count):
    return (jnp.arange(tok_count, dtype=jnp.int32) // BLOCK).astype(jnp.int32)

def slot_layout(counts_row, slot_count, capacity):
    expert_count = counts_row.shape[0]
    expert_ids = jnp.arange(expert_count, dtype=jnp.int32)
    slot_ends = jnp.cumsum(counts_row).astype(jnp.int32)
    starts = (slot_ends - counts_row).astype(jnp.int32)
    slot_ids = jnp.arange(slot_count, dtype=jnp.int32)
    owner_ids = lax.optimization_barrier(jnp.sum((slot_ends[None, :] <= slot_ids[:, None]).astype(jnp.int32), axis=1)).astype(jnp.int32)
    onehot = owner_ids[:, None] == expert_ids[None, :]
    first_slot = lax.optimization_barrier(jnp.sum(jnp.where(onehot, starts[None, :], 0), axis=1)).astype(jnp.int32)
    padded_index = (owner_ids * capacity + slot_ids - first_slot).astype(jnp.int32)
    place_ids = jnp.arange(expert_count * capacity, dtype=jnp.int32)
    expert_of = (place_ids // capacity).astype(jnp.int32)
    position = (place_ids - expert_of * capacity).astype(jnp.int32)
    place_hot = expert_of[:, None] == expert_ids[None, :]
    counts_of = lax.optimization_barrier(jnp.sum(jnp.where(place_hot, counts_row[None, :], 0), axis=1)).astype(jnp.int32)
    starts_of = lax.optimization_barrier(jnp.sum(jnp.where(place_hot, starts[None, :], 0), axis=1)).astype(jnp.int32)
    is_live = position < counts_of
    source = jnp.clip(starts_of + position, 0, slot_count - 1).astype(jnp.int32)
    return (padded_index, is_live, source)

def dispatch_window(normed, slot_keys, reach_row, counts_row):
    tok_count = normed.shape[0]
    slot_count = slot_keys.shape[1]
    capacity = 2 * slot_count // counts_row.shape[0]
    logits = jnp.dot(normed.astype(jnp.float32), slot_keys.astype(jnp.float32), preferred_element_type=jnp.float32)
    allowed = token_levels(tok_count)[:, None] <= block_levels(reach_row, slot_count)[None, :]
    masked = jnp.where(allowed, logits, -jnp.inf)
    exponent = jnp.exp(masked - lax.optimization_barrier(jnp.max(masked, axis=0, keepdims=True)))
    weights = (exponent / lax.optimization_barrier(jnp.sum(exponent, axis=0, keepdims=True))).astype(jnp.bfloat16)
    slot_inputs = lax.dot_general(weights.astype(jnp.float32), normed.astype(jnp.float32), (((0,), (0,)), ((), ())), preferred_element_type=jnp.float32).astype(jnp.bfloat16)
    padded_index, is_live, source = slot_layout(counts_row, slot_count, capacity)
    packed = jnp.where(is_live[:, None], jnp.take(slot_inputs, source, axis=0), jnp.zeros((), jnp.bfloat16))
    return (logits, packed, padded_index)

def combine_window(logits, reach_row, own_out, prior_out, has_prior):
    tok_count, slot_count = logits.shape
    allowed = block_levels(reach_row, slot_count)[None, :] <= token_levels(tok_count)[:, None]
    usable = jnp.logical_or(allowed, has_prior)
    largest = lax.optimization_barrier(jnp.max(jnp.where(usable, logits, -jnp.inf), axis=1, keepdims=True))
    own_exp = jnp.exp(jnp.where(allowed, logits, -jnp.inf) - largest)
    prior_exp = jnp.exp(jnp.where(has_prior, logits, -jnp.inf) - largest)
    denominator = lax.optimization_barrier(jnp.sum(own_exp + prior_exp, axis=1, keepdims=True))
    own_weights = (own_exp / denominator).astype(jnp.bfloat16)
    prior_weights = (prior_exp / denominator).astype(jnp.bfloat16)
    summed = jnp.dot(own_weights.astype(jnp.float32), own_out.astype(jnp.float32), preferred_element_type=jnp.float32)
    summed = summed + jnp.dot(prior_weights.astype(jnp.float32), prior_out.astype(jnp.float32), preferred_element_type=jnp.float32)
    return summed.astype(jnp.bfloat16)

def expert_rows(slot_rows, w_first, w_second):
    hidden = jnp.dot(slot_rows.astype(jnp.float32), w_first.astype(jnp.float32), preferred_element_type=jnp.float32)
    hidden = jax.nn.gelu(hidden, approximate=True).astype(jnp.bfloat16)
    return jnp.dot(hidden.astype(jnp.float32), w_second.astype(jnp.float32), preferred_element_type=jnp.float32).astype(jnp.bfloat16)

def pick_rows(source_rows, positions):
    return jnp.take(source_rows, positions, axis=0)

def reference(tokens, slot_keys, expert_in, expert_out, slot_counts, slot_reach):
    windows = slot_counts.shape[0]
    experts = slot_counts.shape[1]
    model_width = tokens.shape[1]
    normed = normalize(tokens).reshape(windows, -1, model_width)

    def first_pass(members):
        return dispatch_window(members[0], slot_keys, members[1], members[2])
    logits, packed, padded_index = lax.map(first_pass, (normed, slot_reach, slot_counts))
    grouped = jnp.swapaxes(packed.reshape(windows, experts, -1, model_width), 0, 1)

    def apply_expert(members):
        slot_rows, w_first, w_second = members
        flattened = slot_rows.reshape(-1, model_width)
        return expert_rows(flattened, w_first, w_second).reshape(slot_rows.shape)
    produced = lax.map(apply_expert, (grouped, expert_in, expert_out))
    returned = jnp.swapaxes(produced, 0, 1).reshape(windows, -1, model_width)
    own_out = jax.vmap(pick_rows)(returned, padded_index)
    prior_out = jnp.concatenate([jnp.zeros_like(own_out[:1]), own_out[:-1]], axis=0)
    window_ids = jnp.arange(windows, dtype=jnp.int32)

    def second_pass(members):
        logits_window, reach_row, own_rows, prior_rows, window_id = members
        return combine_window(logits_window, reach_row, own_rows, prior_rows, window_id > 0)
    mixed = lax.map(second_pass, (logits, slot_reach, own_out, prior_out, window_ids))
    return mixed.reshape(tokens.shape)
```

```python
import functools

import jax
import jax.numpy as jnp
from jax import lax
from jax.experimental import pallas as pl
from jax.experimental.pallas import tpu as pltpu
from jax.sharding import PartitionSpec as P

BLOCK = 64
EPSILON = 1e-06
MESH = pl.DeviceIdType.MESH
ROWS = 64
PIECES = 4


def iota(shape, dim):
    return lax.broadcasted_iota(jnp.int32, shape, dim)


def dot(a, b):
    return jnp.dot(a, b, preferred_element_type=jnp.float32)


def pick(axis_ids, width, values):
    chosen = jnp.full(axis_ids.shape, values[0], jnp.int32)
    for i in range(1, len(values)):
        chosen = jnp.where(axis_ids >= i * width, values[i], chosen)
    return chosen


def kernel(
    n_ctx, n_exp, counts, reach, tokens, keys, first, second, out,
    first_v, second_v, normed, logits, weights, slot_in, send, recv, prod, ret, place, mix_w, mix_v,
    weight_sem, send_in, recv_in, send_out, recv_out, send_prior, recv_prior,
):
    toks, width = tokens.shape
    slots = keys.shape[1]
    local = first.shape[0]
    hidden = first.shape[2]
    experts = counts.shape[1]
    cap = 2 * slots // experts
    reach_width = slots // reach.shape[1]
    ctx, me = lax.axis_index("ctx"), lax.axis_index("exp")
    window = ctx * n_exp + me
    windows = n_ctx * n_exp
    after = lax.rem(window + 1, windows)
    before = lax.rem(window + windows - 1, windows)

    loads = []
    for j in range(local):
        for source, target, n in ((first, first_v, 0), (second, second_v, 1)):
            load = pltpu.make_async_copy(source.at[j], target.at[j], weight_sem.at[j, n])
            load.start()
            loads.append(load)

    barrier = pltpu.get_barrier_semaphore()
    for o in range(1, n_exp):
        pl.semaphore_signal(
            barrier, inc=1, device_id=(ctx, lax.rem(me + o, n_exp)), device_id_type=MESH
        )
    for other in (after, before):
        pl.semaphore_signal(
            barrier, inc=1, device_id=(other // n_exp, lax.rem(other, n_exp)), device_id_type=MESH
        )

    def normalize(i, carry):
        rows = pl.ds(pl.multiple_of(i * ROWS, ROWS), ROWS)
        floats = tokens[rows, :].astype(jnp.float32)
        scale = lax.rsqrt(jnp.mean(floats * floats, axis=-1, keepdims=True) + EPSILON)
        normed[rows, :] = (floats * scale).astype(jnp.bfloat16)
        return carry

    lax.fori_loop(0, toks // ROWS, normalize, 0)
    logits[...] = dot(normed[...], keys[...])

    slot_level = pick(iota((1, slots), 1), reach_width, [reach[0, b] for b in range(reach.shape[1])])
    for b in range(slots // 128):
        cols = slice(b * 128, (b + 1) * 128)
        allowed = iota((toks, 128), 0) // BLOCK <= slot_level[:, cols]
        masked = jnp.where(allowed, logits[:, cols], -jnp.inf)
        exponent = jnp.exp(masked - jnp.max(masked, axis=0, keepdims=True))
        weights[:, cols] = (exponent / jnp.sum(exponent, axis=0, keepdims=True)).astype(jnp.bfloat16)
    slot_in[...] = lax.dot_general(
        weights[...], normed[...], (((0,), (0,)), ((), ())), preferred_element_type=jnp.float32
    ).astype(jnp.bfloat16)

    taken = [counts[0, e] for e in range(experts)]
    starts = []
    total = jnp.int32(0)
    for e in range(experts):
        starts.append(total)
        total = total + taken[e]

    pl.semaphore_wait(barrier, n_exp + 1)

    group = n_exp * cap
    mine = pl.ds(pl.multiple_of(me * cap, cap), cap)

    def to_expert(j, o):
        peer = lax.rem(me + o, n_exp)
        theirs = pl.ds(pl.multiple_of(peer * cap, cap), cap)
        return pltpu.make_async_remote_copy(
            src_ref=send.at[j, theirs],
            dst_ref=recv.at[j, mine],
            send_sem=send_in.at[j, o],
            recv_sem=recv_in.at[j, o],
            device_id=(ctx, peer),
            device_id_type=MESH,
        )

    def to_home(j, o):
        peer = lax.rem(me + o, n_exp)
        theirs = pl.ds(pl.multiple_of(peer * cap, cap), cap)
        there = pl.ds(pl.multiple_of((me * local + j) * cap, cap), cap)
        return pltpu.make_async_remote_copy(
            src_ref=prod.at[j, theirs],
            dst_ref=ret.at[there],
            send_sem=send_out.at[j, o],
            recv_sem=recv_out.at[j, o],
            device_id=(ctx, peer),
            device_id_type=MESH,
        )

    for j in range(local):
        chosen = [d * local + j for d in range(n_exp)]
        row = iota((group, 1), 0)
        shift = pick(row, cap, [starts[e] - d * cap for d, e in enumerate(chosen)])
        limit = pick(row, cap, [taken[e] + d * cap for d, e in enumerate(chosen)])
        source = jnp.where(row < limit, row + shift, -1)
        hot = jnp.where(iota((group, slots), 1) == source, 1.0, 0.0).astype(jnp.bfloat16)
        send[j] = dot(hot, slot_in[...]).astype(jnp.bfloat16)
        for o in range(1, n_exp):
            to_expert(j, o).start()
        recv[j, mine, :] = send[j, mine, :]

    column = iota((1, experts * cap), 1)
    shift = pick(column, cap, [starts[e] - e * cap for e in range(experts)])
    limit = pick(column, cap, [taken[e] + e * cap for e in range(experts)])
    source = jnp.where(column < limit, column + shift, -1)
    has_prior = window > 0

    def ready(i, carry):
        rows = pl.ds(pl.multiple_of(i * ROWS, ROWS), ROWS)
        slot = iota((ROWS, experts * cap), 0) + i * ROWS
        place[rows, :] = jnp.where(slot == source, 1.0, 0.0).astype(jnp.bfloat16)
        return carry

    lax.fori_loop(0, slots // ROWS, ready, 0)

    def mixing(i, carry):
        rows = pl.ds(pl.multiple_of(i * ROWS, ROWS), ROWS)
        level = (iota((ROWS, slots), 0) + i * ROWS) // BLOCK
        allowed = slot_level <= level
        usable = jnp.logical_or(allowed, has_prior)
        masked = jnp.where(usable, logits[rows, :], -jnp.inf)
        every = jnp.exp(masked - jnp.max(masked, axis=1, keepdims=True))
        own = jnp.where(allowed, every, 0.0)
        prior = jnp.where(has_prior, every, 0.0)
        denominator = jnp.sum(own + prior, axis=1, keepdims=True)
        mix_w[rows, :slots] = (own / denominator).astype(jnp.bfloat16)
        mix_w[rows, slots:] = (prior / denominator).astype(jnp.bfloat16)
        return carry

    lax.fori_loop(0, toks // ROWS, mixing, 0)

    tile = min(512, hidden)

    for j in range(local):
        loads[2 * j].wait()
        loads[2 * j + 1].wait()
        for o in range(1, n_exp):
            to_expert(j, o).wait_recv()
        total_out = None
        for t in range(hidden // tile):
            cols = slice(t * tile, (t + 1) * tile)
            active = jax.nn.gelu(dot(recv[j], first_v[j, :, cols]), approximate=True)
            term = dot(active.astype(jnp.bfloat16), second_v[j, cols, :])
            total_out = term if total_out is None else total_out + term
        prod[j] = total_out.astype(jnp.bfloat16)
        for o in range(1, n_exp):
            to_home(j, o).start()
        here = pl.ds(pl.multiple_of((me * local + j) * cap, cap), cap)
        ret[here, :] = prod[j, mine, :]

    for j in range(local):
        for o in range(1, n_exp):
            to_home(j, o).wait_recv()

    piece = slots // PIECES

    def to_next(p):
        return pltpu.make_async_remote_copy(
            src_ref=mix_v.at[pl.ds(p * piece, piece)],
            dst_ref=mix_v.at[pl.ds(slots + p * piece, piece)],
            send_sem=send_prior.at[p],
            recv_sem=recv_prior.at[p],
            device_id=(after // n_exp, lax.rem(after, n_exp)),
            device_id_type=MESH,
        )

    for p in range(PIECES):
        rows = slice(p * piece, (p + 1) * piece)
        mix_v[rows, :] = dot(place[rows, :], ret[...]).astype(jnp.bfloat16)

        @pl.when(window < windows - 1)
        def _():
            to_next(p).start()

    @pl.when(window == 0)
    def _():
        mix_v[slots:, :] = jnp.zeros((slots, width), jnp.bfloat16)

    @pl.when(window > 0)
    def _():
        for p in range(PIECES):
            to_next(p).wait_recv()

    out[...] = dot(mix_w[...], mix_v[...]).astype(jnp.bfloat16)

    @pl.when(window < windows - 1)
    def _():
        for p in range(PIECES):
            to_next(p).wait_send()

    for j in range(local):
        for o in range(1, n_exp):
            to_expert(j, o).wait_send()
            to_home(j, o).wait_send()


def layer(n_ctx, n_exp, tokens, slot_keys, expert_in, expert_out, slot_counts, slot_reach):
    toks, width = tokens.shape
    slots = slot_keys.shape[1]
    local = expert_in.shape[0]
    experts = slot_counts.shape[1]
    cap = 2 * slots // experts
    bf16, f32 = jnp.bfloat16, jnp.float32
    in_vmem = pl.BlockSpec(memory_space=pltpu.VMEM)
    in_smem = pl.BlockSpec(memory_space=pltpu.SMEM)
    in_any = pl.BlockSpec(memory_space=pl.ANY)
    dma = pltpu.SemaphoreType.DMA
    return pl.pallas_call(
        functools.partial(kernel, n_ctx, n_exp),
        out_shape=jax.ShapeDtypeStruct((toks, width), bf16),
        in_specs=[in_smem, in_smem, in_vmem, in_vmem, in_any, in_any],
        out_specs=in_vmem,
        scratch_shapes=[
            pltpu.VMEM(expert_in.shape, bf16),
            pltpu.VMEM(expert_out.shape, bf16),
            pltpu.VMEM((toks, width), bf16),
            pltpu.VMEM((toks, slots), f32),
            pltpu.VMEM((toks, slots), bf16),
            pltpu.VMEM((slots, width), bf16),
            pltpu.VMEM((local, n_exp * cap, width), bf16),
            pltpu.VMEM((local, n_exp * cap, width), bf16),
            pltpu.VMEM((local, n_exp * cap, width), bf16),
            pltpu.VMEM((experts * cap, width), bf16),
            pltpu.VMEM((slots, experts * cap), bf16),
            pltpu.VMEM((toks, 2 * slots), bf16),
            pltpu.VMEM((2 * slots, width), bf16),
            dma((local, 2)),
            dma((local, n_exp)),
            dma((local, n_exp)),
            dma((local, n_exp)),
            dma((local, n_exp)),
            dma((PIECES,)),
            dma((PIECES,)),
        ],
        compiler_params=pltpu.CompilerParams(
            collective_id=0, has_side_effects=True, vmem_limit_bytes=67043328
        ),
    )(slot_counts, slot_reach, tokens, slot_keys, expert_in, expert_out)


def solution(mesh):
    placed = (
        P(("ctx", "exp"), None),
        P(),
        P("exp", None, None),
        P("exp", None, None),
        P(("ctx", "exp"), None),
        P(("ctx", "exp"), None),
    )
    body = functools.partial(layer, mesh.shape["ctx"], mesh.shape["exp"])
    return jax.shard_map(
        body, mesh=mesh, in_specs=placed, out_specs=P(("ctx", "exp"), None), check_vma=False
    )
```

```python
import functools

import jax
import jax.numpy as jnp
from jax import lax
from jax.experimental import pallas as pl
from jax.experimental.pallas import tpu as pltpu
from jax.sharding import PartitionSpec as P

BLOCK = 64
EPSILON = 1e-06
MESH = pl.DeviceIdType.MESH
ROWS = 64
PIECES = 4


def iota(shape, dim):
    return lax.broadcasted_iota(jnp.int32, shape, dim)


def dot(a, b):
    return jnp.dot(a, b, preferred_element_type=jnp.float32)


def pick(axis_ids, width, values):
    chosen = jnp.full(axis_ids.shape, values[0], jnp.int32)
    for i in range(1, len(values)):
        chosen = jnp.where(axis_ids >= i * width, values[i], chosen)
    return chosen


def kernel(
    n_ctx, n_exp, counts, reach, tokens, keys, first, second, out,
    first_v, second_v, normed, logits, weights, slot_in, send, recv, prod, ret, place, mix_w, mix_v, summed,
    weight_sem, send_in, recv_in, send_out, recv_out, send_prior, recv_prior,
):
    toks, width = tokens.shape
    slots = keys.shape[1]
    local = first.shape[0]
    hidden = first.shape[2]
    experts = counts.shape[1]
    cap = 2 * slots // experts
    reach_width = slots // reach.shape[1]
    ctx, me = lax.axis_index("ctx"), lax.axis_index("exp")
    window = ctx * n_exp + me
    windows = n_ctx * n_exp
    after = lax.rem(window + 1, windows)
    before = lax.rem(window + windows - 1, windows)

    loads = []
    for j in range(local):
        for source, target, n in ((first, first_v, 0), (second, second_v, 1)):
            load = pltpu.make_async_copy(source.at[j], target.at[j], weight_sem.at[j, n])
            load.start()
            loads.append(load)

    barrier = pltpu.get_barrier_semaphore()
    for o in range(1, n_exp):
        pl.semaphore_signal(
            barrier, inc=1, device_id=(ctx, lax.rem(me + o, n_exp)), device_id_type=MESH
        )
    for other in (after, before):
        pl.semaphore_signal(
            barrier, inc=1, device_id=(other // n_exp, lax.rem(other, n_exp)), device_id_type=MESH
        )

    def normalize(i, carry):
        rows = pl.ds(pl.multiple_of(i * ROWS, ROWS), ROWS)
        floats = tokens[rows, :].astype(jnp.float32)
        scale = lax.rsqrt(jnp.mean(floats * floats, axis=-1, keepdims=True) + EPSILON)
        normed[rows, :] = (floats * scale).astype(jnp.bfloat16)
        return carry

    lax.fori_loop(0, toks // ROWS, normalize, 0)
    logits[...] = dot(normed[...], keys[...])

    slot_level = pick(iota((1, slots), 1), reach_width, [reach[0, b] for b in range(reach.shape[1])])
    for b in range(slots // 128):
        cols = slice(b * 128, (b + 1) * 128)
        allowed = iota((toks, 128), 0) // BLOCK <= slot_level[:, cols]
        masked = jnp.where(allowed, logits[:, cols], -jnp.inf)
        exponent = jnp.exp(masked - jnp.max(masked, axis=0, keepdims=True))
        weights[:, cols] = (exponent / jnp.sum(exponent, axis=0, keepdims=True)).astype(jnp.bfloat16)
    slot_in[...] = lax.dot_general(
        weights[...], normed[...], (((0,), (0,)), ((), ())), preferred_element_type=jnp.float32
    ).astype(jnp.bfloat16)

    taken = [counts[0, e] for e in range(experts)]
    starts = []
    total = jnp.int32(0)
    for e in range(experts):
        starts.append(total)
        total = total + taken[e]

    pl.semaphore_wait(barrier, n_exp + 1)

    group = n_exp * cap
    mine = pl.ds(pl.multiple_of(me * cap, cap), cap)

    def to_expert(j, o):
        peer = lax.rem(me + o, n_exp)
        theirs = pl.ds(pl.multiple_of(peer * cap, cap), cap)
        return pltpu.make_async_remote_copy(
            src_ref=send.at[j, theirs],
            dst_ref=recv.at[j, mine],
            send_sem=send_in.at[j, o],
            recv_sem=recv_in.at[j, o],
            device_id=(ctx, peer),
            device_id_type=MESH,
        )

    def to_home(j, o):
        peer = lax.rem(me + o, n_exp)
        theirs = pl.ds(pl.multiple_of(peer * cap, cap), cap)
        there = pl.ds(pl.multiple_of((me * local + j) * cap, cap), cap)
        return pltpu.make_async_remote_copy(
            src_ref=prod.at[j, theirs],
            dst_ref=ret.at[there],
            send_sem=send_out.at[j, o],
            recv_sem=recv_out.at[j, o],
            device_id=(ctx, peer),
            device_id_type=MESH,
        )

    for j in range(local):
        chosen = [d * local + j for d in range(n_exp)]
        row = iota((group, 1), 0)
        shift = pick(row, cap, [starts[e] - d * cap for d, e in enumerate(chosen)])
        limit = pick(row, cap, [taken[e] + d * cap for d, e in enumerate(chosen)])
        source = jnp.where(row < limit, row + shift, -1)
        hot = jnp.where(iota((group, slots), 1) == source, 1.0, 0.0).astype(jnp.bfloat16)
        send[j] = dot(hot, slot_in[...]).astype(jnp.bfloat16)
        for o in range(1, n_exp):
            to_expert(j, o).start()
        recv[j, mine, :] = send[j, mine, :]

    column = iota((1, experts * cap), 1)
    shift = pick(column, cap, [starts[e] - e * cap for e in range(experts)])
    limit = pick(column, cap, [taken[e] + e * cap for e in range(experts)])
    source = jnp.where(column < limit, column + shift, -1)
    has_prior = window > 0

    def ready(i, carry):
        rows = pl.ds(pl.multiple_of(i * ROWS, ROWS), ROWS)
        slot = iota((ROWS, experts * cap), 0) + i * ROWS
        place[rows, :] = jnp.where(slot == source, 1.0, 0.0).astype(jnp.bfloat16)
        return carry

    lax.fori_loop(0, slots // ROWS, ready, 0)

    def mixing(i, carry):
        rows = pl.ds(pl.multiple_of(i * ROWS, ROWS), ROWS)
        level = (iota((ROWS, slots), 0) + i * ROWS) // BLOCK
        allowed = slot_level <= level
        usable = jnp.logical_or(allowed, has_prior)
        masked = jnp.where(usable, logits[rows, :], -jnp.inf)
        every = jnp.exp(masked - jnp.max(masked, axis=1, keepdims=True))
        own = jnp.where(allowed, every, 0.0)
        prior = jnp.where(has_prior, every, 0.0)
        denominator = jnp.sum(own + prior, axis=1, keepdims=True)
        mix_w[rows, :slots] = (own / denominator).astype(jnp.bfloat16)
        mix_w[rows, slots:] = (prior / denominator).astype(jnp.bfloat16)
        return carry

    lax.fori_loop(0, toks // ROWS, mixing, 0)

    tile = min(512, hidden)

    for j in range(local):
        loads[2 * j].wait()
        loads[2 * j + 1].wait()
        for o in range(1, n_exp):
            to_expert(j, o).wait_recv()
        total_out = None
        for t in range(hidden // tile):
            cols = slice(t * tile, (t + 1) * tile)
            active = jax.nn.gelu(dot(recv[j], first_v[j, :, cols]), approximate=True)
            term = dot(active.astype(jnp.bfloat16), second_v[j, cols, :])
            total_out = term if total_out is None else total_out + term
        prod[j] = total_out.astype(jnp.bfloat16)
        for o in range(1, n_exp):
            to_home(j, o).start()
        here = pl.ds(pl.multiple_of((me * local + j) * cap, cap), cap)
        ret[here, :] = prod[j, mine, :]

    for j in range(local):
        for o in range(1, n_exp):
            to_home(j, o).wait_recv()

    piece = slots // PIECES

    def to_next(p):
        return pltpu.make_async_remote_copy(
            src_ref=mix_v.at[pl.ds(p * piece, piece)],
            dst_ref=mix_v.at[pl.ds(slots + p * piece, piece)],
            send_sem=send_prior.at[p],
            recv_sem=recv_prior.at[p],
            device_id=(after // n_exp, lax.rem(after, n_exp)),
            device_id_type=MESH,
        )

    for p in range(PIECES):
        rows = slice(p * piece, (p + 1) * piece)
        mix_v[rows, :] = dot(place[rows, :], ret[...]).astype(jnp.bfloat16)

        @pl.when(window < windows - 1)
        def _():
            to_next(p).start()

    @pl.when(window == 0)
    def _():
        mix_v[slots:, :] = jnp.zeros((slots, width), jnp.bfloat16)

    def mix(first_col, last_col):
        cols = slice(first_col, last_col)
        return dot(mix_w[:, cols], mix_v[cols, :])

    def arrived(p):
        @pl.when(window > 0)
        def _():
            to_next(p).wait_recv()

    summed[...] = mix(0, slots)
    late = slots + (PIECES - 1) * piece
    for p in range(PIECES - 1):
        arrived(p)
    summed[...] += mix(slots, late)
    arrived(PIECES - 1)
    out[...] = (summed[...] + mix(late, 2 * slots)).astype(jnp.bfloat16)

    @pl.when(window < windows - 1)
    def _():
        for p in range(PIECES):
            to_next(p).wait_send()

    for j in range(local):
        for o in range(1, n_exp):
            to_expert(j, o).wait_send()
            to_home(j, o).wait_send()


def layer(n_ctx, n_exp, tokens, slot_keys, expert_in, expert_out, slot_counts, slot_reach):
    toks, width = tokens.shape
    slots = slot_keys.shape[1]
    local = expert_in.shape[0]
    experts = slot_counts.shape[1]
    cap = 2 * slots // experts
    bf16, f32 = jnp.bfloat16, jnp.float32
    in_vmem = pl.BlockSpec(memory_space=pltpu.VMEM)
    in_smem = pl.BlockSpec(memory_space=pltpu.SMEM)
    in_any = pl.BlockSpec(memory_space=pl.ANY)
    dma = pltpu.SemaphoreType.DMA
    return pl.pallas_call(
        functools.partial(kernel, n_ctx, n_exp),
        out_shape=pltpu.VMEM((toks, width), bf16),
        in_specs=[in_smem, in_smem, in_vmem, in_vmem, in_any, in_any],
        out_specs=in_vmem,
        scratch_shapes=[
            pltpu.VMEM(expert_in.shape, bf16),
            pltpu.VMEM(expert_out.shape, bf16),
            pltpu.VMEM((toks, width), bf16),
            pltpu.VMEM((toks, slots), f32),
            pltpu.VMEM((toks, slots), bf16),
            pltpu.VMEM((slots, width), bf16),
            pltpu.VMEM((local, n_exp * cap, width), bf16),
            pltpu.VMEM((local, n_exp * cap, width), bf16),
            pltpu.VMEM((local, n_exp * cap, width), bf16),
            pltpu.VMEM((experts * cap, width), bf16),
            pltpu.VMEM((slots, experts * cap), bf16),
            pltpu.VMEM((toks, 2 * slots), bf16),
            pltpu.VMEM((2 * slots, width), bf16),
            pltpu.VMEM((toks, width), f32),
            dma((local, 2)),
            dma((local, n_exp)),
            dma((local, n_exp)),
            dma((local, n_exp)),
            dma((local, n_exp)),
            dma((PIECES,)),
            dma((PIECES,)),
        ],
        compiler_params=pltpu.CompilerParams(
            collective_id=0, has_side_effects=True, vmem_limit_bytes=60*2**20
        ),
    )(slot_counts, slot_reach, tokens, slot_keys, expert_in, expert_out)


def solution(mesh):
    placed = (
        P(("ctx", "exp"), None),
        P(),
        P("exp", None, None),
        P("exp", None, None),
        P(("ctx", "exp"), None),
        P(("ctx", "exp"), None),
    )
    body = functools.partial(layer, mesh.shape["ctx"], mesh.shape["exp"])
    return jax.shard_map(
        body, mesh=mesh, in_specs=placed, out_specs=P(("ctx", "exp"), None), check_vma=False
    )
```
